32 devices in a mesh: tbl: 16 (over z, x, core), hst: 2 (over y).
Axes of the slice: x: 2, y: 2, z: 4, core: 2. Of those that a mesh axis runs over, the one named last changes fastest.
Arguments:
- pooled: bfloat16 [8192, 512], P('tbl'), may hold values from -6 to 6
- w_up: bfloat16 [512, 4096], P(None, 'hst'), may hold values from -0.25 to 0.25
- grad_out: bfloat16 [8192, 4096], P('tbl', 'hst'), may hold values from -6 to 6
- owners: int32 [4, 8192, 8], P('hst', 'tbl'), may hold values from 0 to 15, all different within a row; in each aligned block of 512 rows (0 to 511, 512 to 1023, ..., all dimensions but the last counted through in order) at most 512 rows name the same one
- rows: int32 [4, 8192, 8], P('hst', 'tbl'), may hold values from 0 to 1023
- lookup_weight: bfloat16 [4, 8192, 8], P('hst', 'tbl'), may hold values from 0.25 to 2
- lens: int32 [4, 8192], P('hst', 'tbl'), may hold values from 4 to 8
- slot_map: int32 [16, 2, 2048], P('tbl', 'hst'), may hold values from 0 to 2047, each once within a row
- cache_weight: float32 [16, 2, 2048, 128], P('tbl', 'hst'), may hold values from -6 to 6
- cache_accum: float32 [16, 2, 2048], P('tbl', 'hst'), may hold values from 0.1 to 10
- evict_slots: int32 [16, 2, 256], P('tbl', 'hst'), may hold values from 0 to 2047, as said below
- evict_dest: int32 [16, 2, 256], P('tbl', 'hst'), may hold values from 0 to 1, as said below
- evict_count: int32 [16, 2], P('tbl', 'hst'), may hold values from 128 to 256
Outputs:
- grad_up: float32 [512, 4096], P('tbl', 'hst')
- new_weight: float32 [16, 2, 2048, 128], P('tbl', 'hst')
- new_accum: float32 [16, 2, 2048], P('tbl', 'hst')
- held_rows: float32 [16, 2, 2, 128, 128], P('tbl', 'hst')
- held_accum: float32 [16, 2, 2, 128], P('tbl', 'hst')
The draws below stay inside these ranges and needn't reach their ends.
Inputs may be any that keep to these rules, and one draw needn't show every extreme that they name: The 8 owners of one bag differ. Among the 512 samples of one index of tbl and one table, no owner is named by more than 512 lookup positions, used or not; some owner is named by exactly 512 in some such block. `evict_slots`: the 256 slots of one device's list differ. `evict_dest`: among the used entries of one device, no holder appears more than 128 times, and one holder appears exactly 128 times.
All inputs are finite; a program needn't handle non-finite values.
Results may differ from the reference program's by a relative error of at most 0.0029.
Values may be sent and summed in bfloat16 or wider, within the bound.
A program may use at most 64 MiB of HBM per device.

```python
import math
import jax
import jax.numpy as jnp
import numpy as np
from jax import lax

EMB = 128
HIDDEN_SIZE = 4096
TABLES_DEV = 2
BAG = 8
B_DEV = 512
ROWS_DEV = 1024
EVICT = 256
OWNERS = 16
HOLDERS = 2
B = 8192
TABLES = 4
FEAT = 512
SLOTS = 2048
CAP = 128
MOST = 512


def eviction_plan(key):
    keys = jax.random.split(jax.random.fold_in(key, 7), 4)
    devices = OWNERS * HOLDERS
    amounts = jax.random.randint(keys[0], (devices,), CAP, EVICT + 1)
    favored = jax.random.randint(keys[1], (devices,), 0, HOLDERS)
    offsets = jax.random.randint(keys[2], (devices, EVICT), 1, HOLDERS)
    positions = jnp.arange(EVICT, dtype=jnp.int32)
    baseline = jnp.where(positions[None, :] < CAP, favored[:, None], (favored[:, None] + offsets) % HOLDERS)
    scores = jax.random.randint(keys[3], (devices, EVICT), 0, 1 << 20)
    sorting = jnp.where(positions[None, :] < amounts[:, None], scores * EVICT + positions[None, :], (1 << 30) + positions[None, :])
    arrange = jnp.argsort(sorting, axis=1, stable=True)
    targets = jnp.take_along_axis(baseline, arrange, axis=1)
    return (targets.reshape(OWNERS, HOLDERS, EVICT).astype(jnp.int32), amounts.reshape(OWNERS, HOLDERS).astype(jnp.int32))


def draw_evict_dest(key, part):
    return eviction_plan(key)[0]


def draw_evict_count(key, part):
    return eviction_plan(key)[1]


def draw_evict_slots(key, part):
    keys = jax.random.split(jax.random.fold_in(key, 11), OWNERS * HOLDERS)
    chosen = jax.vmap(lambda single: jax.random.permutation(single, SLOTS)[:EVICT])(keys)
    return chosen.reshape(OWNERS, HOLDERS, EVICT).astype(jnp.int32)


def plant(array, own_key, low, top_value):
    extent = array.shape
    spot = [jax.random.randint(jax.random.fold_in(own_key, axis), (), 0, extent[axis]) for axis in range(len(extent))]
    array = array.at[tuple(spot)].set(low)
    longest = extent.index(max(extent))
    spot[longest] = (spot[longest] + 1) % extent[longest]
    return array.at[tuple(spot)].set(top_value)


def strengthened(entries, own_key, source, target, blocks, factor):
    def block_of(position):
        return (jnp.arange(entries.shape[position]) // (entries.shape[position] // blocks)).reshape((-1,) + (1,) * (entries.ndim - 1 - position))

    near = jax.random.permutation(own_key, blocks)[block_of(target)]
    second = (block_of(target) + blocks // 2) % blocks
    return jnp.where((block_of(source) == near) | (block_of(source) == second), factor * entries, entries)


def steps_of(stream_key, shape, cuts, smallest, top_value):
    factor_of = 1.0
    for axis_at, blocks in cuts:
        steps = jax.random.uniform(jax.random.fold_in(jax.random.fold_in(stream_key, 6), axis_at), (blocks,), jnp.float32, smallest / len(cuts), top_value / len(cuts))
        factor_of = factor_of * jnp.repeat(jnp.exp(steps), shape[axis_at] // blocks).reshape((-1,) + (1,) * (len(shape) - 1 - axis_at))
    return factor_of


def assign_block(rng, own, number, rows, amount, top, bound, skew):
    sequence = jax.random.permutation(rng, amount)
    heavy_load, usual = shares(amount, rows * top, bound, skew, True), shares(amount, rows * top, bound, skew, False)
    places = jnp.arange(amount)

    def named(lengths, rotation):
        used = int((lengths > 0).sum())
        fixed = max(1, used // 4)
        passed = fixed + (places - fixed + rotation * (used - fixed)) % max(1, amount - fixed)
        return jnp.zeros((amount,), jnp.int32).at[sequence[jnp.where(places < fixed, places, passed)]].set(jnp.asarray(lengths, jnp.int32))

    lengths = jnp.where(number % 4 == 0, named(heavy_load, number // 4), named(usual, number - number // 4 - 1))
    mixed = jax.random.permutation(jax.random.fold_in(own, 3), amount)
    giver, receiver = mixed[0:amount // 2 * 2:2], mixed[1:amount // 2 * 2:2]
    slack = jnp.minimum(lengths[giver] - 1, bound - lengths[receiver]) // 2
    slack = jnp.where((giver == sequence[0]) | (receiver == sequence[0]) | (lengths[receiver] == 0), 0, jnp.maximum(slack, 0))
    passed = jax.random.randint(jax.random.fold_in(own, 4), (amount // 2,), 0, 1 << 20) % (slack + 1)
    lengths = lengths.at[giver].add(-passed).at[receiver].add(passed)
    members = jnp.searchsorted(jnp.cumsum(lengths), jnp.arange(rows * top), side="right").astype(jnp.int32)
    grid = members.reshape(top, rows).T
    grid = grid[jax.random.permutation(jax.random.fold_in(own, 1), rows)]
    rotation = jax.random.randint(jax.random.fold_in(own, 2), (rows, 1), 0, top)
    return jnp.take_along_axis(grid, (jnp.arange(top)[None, :] + rotation) % top, axis=1)


def shares(number_of, total, bound, slope, full):
    portions = [(1 << 20) // math.isqrt(rank ** slope) + 1 for rank in range(1, number_of + 1)]
    largest = bound if full else min(bound, max(-(-total // number_of), total * portions[0] // sum(portions)))
    least = 1 if total - largest >= number_of - 1 else 0
    given, rest = [largest] + [least] * (number_of - 1), total - largest - least * (number_of - 1)
    while rest > 0:
        candidates = [i for i in range(1, number_of) if given[i] < largest] or [i for i in range(1, number_of) if given[i] < bound]
        mass, budget = sum([portions[i] for i in candidates]), rest
        for i in candidates:
            extra = min(bound - given[i], max(1, budget * portions[i] // mass), rest)
            given[i] = given[i] + extra
            rest = rest - extra
    return np.array(given)


def gaussian(key, extent, scale, bound, cuts=(), held_as=jnp.bfloat16):
    values = scale * jax.random.normal(key, extent, jnp.float32)
    if cuts:
        values = values * steps_of(key, extent, cuts, -0.22, 0.18)
    return jnp.clip(values, -bound, bound).astype(held_as)


def bell_draw_with(key, extent, width, limit, cuts, heavy, held_as=jnp.bfloat16):
    result = width * jax.random.normal(key, extent, jnp.float32)
    if cuts:
        result = result * steps_of(key, extent, cuts, -0.22, 0.18)
    return jnp.clip(strengthened(result, jax.random.fold_in(key, 3), *heavy), -limit, limit).astype(held_as)


def setup_inputs(seed: int = 0) -> dict:
    streams_of = jax.random.split(jax.random.key(seed), 14)
    pooled = bell_draw_with(streams_of[0], (B, FEAT), 1.0, 6.0, ((0, 16),), (0, 1, 16, 2.0))
    w_up = gaussian(streams_of[1], (FEAT, HIDDEN_SIZE), FEAT ** -0.5, 0.25, ((1, 2),))
    grad_out = gaussian(streams_of[2], (B, HIDDEN_SIZE), 1.0, 6.0, ((0, 16), (1, 2)))
    owners_keys = jax.random.split(jax.random.fold_in(streams_of[3], 1), TABLES * B // B_DEV)
    owners_turns = jax.random.permutation(jax.random.fold_in(streams_of[3], 3), TABLES * B // B_DEV)
    owners = jax.vmap(lambda own, number: assign_block(jax.random.fold_in(streams_of[3], 2), own, number, B_DEV, OWNERS, BAG, MOST, 1))(owners_keys, owners_turns).reshape((TABLES, B, BAG))
    rows = plant(jax.random.randint(streams_of[4], (TABLES, B, BAG), 0, ROWS_DEV), jax.random.fold_in(streams_of[4], 1), 0, ROWS_DEV - 1).astype(jnp.int32)
    lookup_weight = jnp.clip(jnp.exp(math.log(2.0) - 2.0794415 * jax.random.uniform(streams_of[5], (TABLES, B, BAG), jnp.float32) ** steps_of(streams_of[5], (TABLES, B, BAG), ((0, 2), (1, 16)), -0.2, 0.2)), 0.25, 2.0).astype(jnp.bfloat16)
    lens = plant(jax.random.randint(streams_of[6], (TABLES, B), (BAG + 1) // 2, BAG + 1), jax.random.fold_in(streams_of[6], 1), (BAG + 1) // 2, BAG).astype(jnp.int32)
    slot_map = jax.vmap(lambda own: jax.random.permutation(own, SLOTS))(jax.random.split(streams_of[7], OWNERS * HOLDERS)).reshape((OWNERS, HOLDERS, SLOTS)).astype(jnp.int32)
    cache_weight = gaussian(streams_of[8], (OWNERS, HOLDERS, SLOTS, EMB), 1.0, 6.0, ((0, 16), (1, 2)), jnp.float32)
    cache_accum = jnp.clip(jnp.exp(math.log(10.0) - 4.6051702 * jax.random.uniform(streams_of[9], (OWNERS, HOLDERS, SLOTS), jnp.float32) ** steps_of(streams_of[9], (OWNERS, HOLDERS, SLOTS), ((0, 16), (1, 2)), -0.2, 0.2)), 0.1, 10.0)
    evict_slots = draw_evict_slots(jax.random.fold_in(streams_of[13], 71), 0)
    evict_dest = draw_evict_dest(jax.random.fold_in(streams_of[13], 71), 0)
    evict_count = draw_evict_count(jax.random.fold_in(streams_of[13], 71), 0)
    return {"pooled": pooled, "w_up": w_up, "grad_out": grad_out, "owners": owners, "rows": rows, "lookup_weight": lookup_weight, "lens": lens, "slot_map": slot_map, "cache_weight": cache_weight, "cache_accum": cache_accum, "evict_slots": evict_slots, "evict_dest": evict_dest, "evict_count": evict_count}


LEARN_RATE = 0.05
EPSILON = 1e-08

def reference(pooled, w_up, grad_out, owners, rows, lookup_weight, lens, slot_map, cache_weight, cache_accum, evict_slots, evict_dest, evict_count):
    preact = jnp.dot(pooled, w_up, preferred_element_type=jnp.float32)
    sigmoid_z = jax.nn.sigmoid(preact)
    delta = (grad_out.astype(jnp.float32) * sigmoid_z * (1.0 + preact * (1.0 - sigmoid_z))).astype(jnp.bfloat16)
    grad_up = lax.dot_general(pooled, delta, (((0,), (0,)), ((), ())), preferred_element_type=jnp.float32)
    feature_grad = lax.dot_general(delta, w_up, (((1,), (1,)), ((), ())), preferred_element_type=jnp.float32)
    bag_grad = feature_grad.astype(jnp.bfloat16).reshape(B, TABLES, EMB)
    bag_major = jnp.transpose(bag_grad, (1, 0, 2)).astype(jnp.float32)
    positions = jnp.arange(BAG, dtype=jnp.int32)
    used = positions[None, None, :] < lens[:, :, None]
    flat_size = OWNERS * HOLDERS * SLOTS

    def one_table(running, table):
        group = table // TABLES_DEV
        local_table = table % TABLES_DEV
        own_rows = owners[table]
        slot_index = slot_map[own_rows, group, local_table * ROWS_DEV + rows[table]]
        flat_index = (own_rows * HOLDERS + group) * SLOTS + slot_index
        flat_index = jnp.where(used[table], flat_index, flat_size).astype(jnp.int32)
        scaled = (lookup_weight[table].astype(jnp.float32)[:, :, None] * bag_major[table][:, None, :]).astype(jnp.bfloat16)
        scaled = lax.optimization_barrier(scaled).astype(jnp.float32)
        running = running.at[flat_index.reshape(-1)].add(scaled.reshape(-1, EMB), mode='drop')
        return (running, None)
    slot_grad, _ = lax.scan(one_table, jnp.zeros((flat_size, EMB), jnp.float32), jnp.arange(TABLES, dtype=jnp.int32))
    slot_grad = slot_grad.reshape(OWNERS, HOLDERS, SLOTS, EMB)
    new_accum = cache_accum + lax.optimization_barrier(jnp.mean(slot_grad * slot_grad, axis=-1))
    new_weight = cache_weight - LEARN_RATE * slot_grad / (jnp.sqrt(new_accum)[..., None] + EPSILON)
    leaving = jnp.take_along_axis(new_weight, evict_slots[..., None], axis=2)
    leaving_accum = jnp.take_along_axis(new_accum, evict_slots, axis=2)
    live = jnp.arange(EVICT, dtype=jnp.int32)[None, None, :] < evict_count[:, :, None]
    picks = ((evict_dest[..., None] == jnp.arange(HOLDERS, dtype=jnp.int32)) & live[..., None]).astype(jnp.int32)
    placed = lax.optimization_barrier(jnp.sum((jnp.cumsum(picks, axis=2) - 1) * picks, axis=-1))
    device_index = jnp.arange(OWNERS, dtype=jnp.int32)[:, None] * HOLDERS + jnp.arange(HOLDERS, dtype=jnp.int32)[None, :]
    goal = device_index[:, :, None] * (HOLDERS * CAP) + evict_dest * CAP + placed
    goal = jnp.where(live, goal, OWNERS * HOLDERS * HOLDERS * CAP).astype(jnp.int32)
    held_flat = jnp.zeros((OWNERS * HOLDERS * HOLDERS * CAP, EMB), jnp.float32).at[goal.reshape(-1)].set(leaving.reshape(-1, EMB), mode='drop')
    accum_flat = jnp.zeros((OWNERS * HOLDERS * HOLDERS * CAP,), jnp.float32).at[goal.reshape(-1)].set(leaving_accum.reshape(-1), mode='drop')
    held_rows = jnp.transpose(held_flat.reshape(OWNERS, HOLDERS, HOLDERS, CAP, EMB), (0, 2, 1, 3, 4))
    held_accum = jnp.transpose(accum_flat.reshape(OWNERS, HOLDERS, HOLDERS, CAP), (0, 2, 1, 3))
    return (grad_up, new_weight, new_accum, held_rows, held_accum)
```

```python
import functools

import jax
import jax.numpy as jnp
from jax import lax
from jax.experimental import pallas as pl
from jax.experimental.pallas import tpu as pltpu
from jax.sharding import PartitionSpec as P

LEARN_RATE = 0.05
EPSILON = 1e-08
MESH = pl.DeviceIdType.MESH
F32 = jnp.float32
BF16 = jnp.bfloat16


def exchange_kernel(
    nz, nx, nh, tables, rows_dev,
    feat, grad, idx,
    grad_out_ref, place_ref,
    ybuf, gat, idxb, rcore, a1, rx, a2, rz,
    y_s, y_r, i_s, i_r, az_s, ax_s, ac_s, g_r, rc_s, rc_r, rx_s, rx_r, rz_s, rz_r,
):
    n = nz * nx * 2
    me = lax.axis_index("tbl")
    h = lax.axis_index("hst")
    c = lax.rem(me, 2)
    zx = me // 2
    x = lax.rem(zx, nx)
    z = zx // nx
    other = 1 - c
    width = ybuf.shape[-1]
    emb = width // tables

    def at(zi, xi, ci):
        return (zi * nx + xi) * 2 + ci

    def zof(d):
        return lax.rem(z + d, nz)

    def xof(d):
        return lax.rem(x + d, nx)

    def rcopy(src, dst, s, r, dev):
        return pltpu.make_async_remote_copy(
            src_ref=src, dst_ref=dst, send_sem=s, recv_sem=r,
            device_id=dev, device_id_type=MESH,
        )

    barrier = pltpu.get_barrier_semaphore()

    def greet(d, carry):
        pl.semaphore_signal(
            barrier, inc=1, device_id={"tbl": lax.rem(me + d, n)}, device_id_type=MESH
        )
        return carry

    lax.fori_loop(1, n, greet, 0)
    for d in range(1, nh):
        pl.semaphore_signal(
            barrier, inc=1, device_id={"hst": lax.rem(h + d, nh)}, device_id_type=MESH
        )
    pl.semaphore_wait(barrier, n - 1 + nh - 1)

    def cols(hh):
        return pl.ds(pl.multiple_of(hh * width, width), width)

    def y_copy(d):
        h2 = lax.rem(h + d, nh)
        return rcopy(feat.at[:, cols(h2)], ybuf.at[h], y_s.at[d], y_r.at[h], {"hst": h2})

    def y_arrival(d):
        h2 = lax.rem(h + d, nh)
        return rcopy(feat.at[:, cols(h2)], ybuf.at[h2], y_s.at[d], y_r.at[h2], {"hst": h2})

    def core_copy(x2):
        return rcopy(
            grad.at[:, x2, other], rcore.at[:, x2], rc_s.at[x2], rc_r.at[x2],
            {"tbl": at(z, x, other)},
        )

    def i_copy(d):
        o = lax.rem(me + d, n)
        return rcopy(idx.at[o], idxb.at[me], i_s.at[d], i_r.at[me], {"tbl": o})

    def i_arrival(slot):
        return rcopy(idx.at[slot], idxb.at[slot], i_s.at[0], i_r.at[slot], {"tbl": at(z, x, other)})

    for d in range(1, nh):
        y_copy(d).start()
    for d in range(1, nx + 1):
        core_copy(xof(d)).start()

    def i_start(d, carry):
        i_copy(d).start()
        return carry

    lax.fori_loop(1, n, i_start, 0)

    def rx_copy(d):
        x2 = xof(d)
        return rcopy(a1.at[:, x2], rx.at[x], rx_s.at[x2], rx_r.at[x], {"tbl": at(z, x2, c)})

    def rx_arrival(d):
        x2 = xof(d)
        return rcopy(a1.at[:, x2], rx.at[x2], rx_s.at[x2], rx_r.at[x2], {"tbl": at(z, x2, c)})

    for d in range(1, nx):
        x2 = xof(d)
        core_copy(x2).wait_recv()

        def add_core(k, carry):
            a1[k, x2] = (grad[k, x2, c].astype(F32) + rcore[k, x2].astype(F32)).astype(BF16)
            return carry

        lax.fori_loop(0, nz, add_core, 0)
        rx_copy(d).start()

    for d in range(1, nh):
        y_arrival(d).wait_recv()
    total = feat[:, cols(h)].astype(F32)
    for d in range(1, nh):
        total = total + ybuf[lax.rem(h + d, nh)].astype(F32)
    gat[me] = total.astype(BF16)

    def g_copy(slot, sem, dev):
        return rcopy(gat.at[slot], gat.at[slot], sem, g_r.at[slot], {"tbl": dev})

    def z_copy(d):
        return g_copy(me, az_s.at[d], at(zof(d), x, c))

    def x_copy(zi, d):
        return g_copy(at(zi, x, c), ax_s.at[zi, d], at(z, xof(d), c))

    def c_copy(zi, xi):
        return g_copy(at(zi, xi, c), ac_s.at[zi, xi], at(z, x, other))

    def arrived(slot):
        g_copy(slot, ac_s.at[0, 0], at(z, x, other)).wait_recv()

    for d in range(1, nx):
        x_copy(z, d).start()

    def z_start(d, carry):
        z_copy(d).start()
        return carry

    lax.fori_loop(1, nz, z_start, 0)
    c_copy(z, x).start()

    place_ref[...] = jnp.zeros_like(place_ref)
    idxb[me] = idx[me]
    chunk = min(256, rows_dev)
    batch = gat.shape[1]

    def proc(slot):
        meta = idxb[slot]
        block = gat[slot]
        for t in range(tables):
            row = meta[t : t + 1, :]
            wgt = meta[tables + t : tables + t + 1, :]
            part = block[:, t * emb : (t + 1) * emb]
            for r0 in range(0, rows_dev, chunk):
                ids = lax.broadcasted_iota(jnp.int32, (chunk, batch), 0).astype(F32) + float(r0)
                mark = jnp.where(ids == row, wgt, 0.0).astype(BF16)
                place_ref[pl.ds(t * rows_dev + r0, chunk), :] += jnp.dot(
                    mark, part, preferred_element_type=F32
                )

    proc(me)

    def z_body(d, carry):
        zi = zof(d)
        slot = at(zi, x, c)
        arrived(slot)
        for dx in range(1, nx):
            x_copy(zi, dx).start()
        c_copy(zi, x).start()
        i_arrival(slot).wait_recv()
        proc(slot)
        return carry

    lax.fori_loop(1, nz, z_body, 0)

    core_copy(x).wait_recv()
    for d in range(1, nx):
        rx_arrival(d).wait_recv()

    def own_sum(k):
        s = grad[k, x, c].astype(F32) + rcore[k, x].astype(F32)
        for d in range(1, nx):
            s = s + rx[xof(d), k].astype(F32)
        return s

    def rz_copy(d):
        zi = zof(d)
        return rcopy(a2.at[zi], rz.at[z], rz_s.at[d], rz_r.at[z], {"tbl": at(zi, x, c)})

    def rz_arrival(d):
        zi = zof(d)
        return rcopy(a2.at[zi], rz.at[zi], rz_s.at[d], rz_r.at[zi], {"tbl": at(zi, x, c)})

    def rz_start(d, carry):
        zi = zof(d)
        a2[zi] = own_sum(zi).astype(BF16)
        rz_copy(d).start()
        return carry

    lax.fori_loop(1, nz, rz_start, 0)

    def x_body(k, carry):
        zi = zof(k // (nx - 1))
        xi = xof(1 + lax.rem(k, nx - 1))
        slot = at(zi, xi, c)
        arrived(slot)
        c_copy(zi, xi).start()
        i_arrival(slot).wait_recv()
        proc(slot)
        return carry

    if nx > 1:
        lax.fori_loop(0, nz * (nx - 1), x_body, 0)

    def c_body(k, carry):
        j = k // nz
        zi = zof(lax.rem(k, nz))
        slot = at(zi, xof(j), other)
        arrived(slot)
        i_arrival(slot).wait_recv()
        proc(slot)
        return carry

    lax.fori_loop(0, nz * nx, c_body, 0)

    grad_out_ref[...] = own_sum(z)

    def rz_end(d, carry):
        rz_arrival(d).wait_recv()
        grad_out_ref[...] += rz[zof(d)].astype(F32)
        return carry

    lax.fori_loop(1, nz, rz_end, 0)

    for d in range(1, nh):
        y_copy(d).wait_send()
    for d in range(1, nx + 1):
        core_copy(xof(d)).wait_send()
    for d in range(1, nx):
        rx_copy(d).wait_send()

    def i_end(d, carry):
        i_copy(d).wait_send()
        return carry

    lax.fori_loop(1, n, i_end, 0)

    def z_end(d, carry):
        z_copy(d).wait_send()
        rz_copy(d).wait_send()
        return carry

    lax.fori_loop(1, nz, z_end, 0)

    def end_all(k, carry):
        for dx in range(1, nx):
            x_copy(k, dx).wait_send()
        for xi in range(nx):
            c_copy(k, xi).wait_send()
        return carry

    lax.fori_loop(0, nz, end_all, 0)


def update_kernel(
    slot_map, evict_slots, goal, place, weight, accum,
    new_weight, new_accum, send_rows, send_accum,
    sgrad, wide,
):
    slots = place.shape[0]
    list_len = evict_slots.shape[0]
    keep = send_accum.shape[0] * send_accum.shape[1]
    step = 16

    def scatter(i, carry):
        for j in range(step):
            r = i * step + j
            sgrad[pl.ds(slot_map[r], 1), :] = place[pl.ds(r, 1), :]
        return carry

    lax.fori_loop(0, slots // step, scatter, 0)
    tile = 128

    def adagrad(i, carry):
        at = pl.ds(i * tile, tile)
        g = sgrad[at, :]
        acc = accum[pl.ds(i, 1), :] + jnp.mean(g * g, axis=-1)[None, :]
        new_accum[pl.ds(i, 1), :] = acc
        col = jnp.broadcast_to(acc.reshape(tile, 1), g.shape)
        wide[at, :] = col
        new_weight[at, :] = weight[at, :] - LEARN_RATE * g / (jnp.sqrt(col) + EPSILON)
        return carry

    lax.fori_loop(0, slots // tile, adagrad, 0)
    send_rows[...] = jnp.zeros_like(send_rows)
    sgrad[...] = jnp.zeros_like(sgrad)

    def evict(i, carry):
        for j in range(8):
            p = i * 8 + j
            s = evict_slots[p]
            k = goal[p]
            send_rows[pl.ds(k, 1), :] = new_weight[pl.ds(s, 1), :]
            sgrad[pl.ds(k, 1), :] = wide[pl.ds(s, 1), :]
        return carry

    lax.fori_loop(0, list_len // 8, evict, 0)
    groups = send_accum.shape[0]
    cap = keep // groups
    for d in range(groups):
        send_accum[d : d + 1, :] = jnp.max(sgrad[d * cap : (d + 1) * cap, :], axis=-1)[None, :]


def on_device(
    nz, nx,
    pooled, w_up, grad_out, owners, rows, lookup_weight, lens, slot_map,
    cache_weight, cache_accum, evict_slots, evict_dest, evict_count,
):
    tables, batch, bag_len = owners.shape
    slots = slot_map.shape[-1]
    rows_dev = slots // tables
    emb = cache_weight.shape[-1]
    n = lax.axis_size("tbl")
    nh = lax.axis_size("hst")
    feat_n, hid = w_up.shape
    out_rows = feat_n // n
    width = tables * emb

    preact = jnp.dot(pooled, w_up, preferred_element_type=F32)
    sig = jax.nn.sigmoid(preact)
    delta = (grad_out.astype(F32) * sig * (1.0 + preact * (1.0 - sig))).astype(BF16)
    feat = lax.dot_general(
        delta, w_up, (((1,), (1,)), ((), ())), preferred_element_type=F32
    ).astype(BF16)
    grad = lax.dot_general(
        pooled, delta, (((0,), (0,)), ((), ())), preferred_element_type=F32
    ).astype(BF16)
    grad = grad.reshape(nz, nx, 2, out_rows, hid)

    own_t = jnp.transpose(owners, (2, 0, 1))
    row_t = jnp.transpose(rows, (2, 0, 1)).astype(F32)
    wgt_t = jnp.transpose(lookup_weight, (2, 0, 1)).astype(F32)
    used = jnp.arange(bag_len, dtype=jnp.int32)[:, None, None] < lens[None]
    hit = (own_t[None] == jnp.arange(n, dtype=jnp.int32)[:, None, None, None]) & used[None]
    row_to = jnp.sum(jnp.where(hit, row_t[None] + 1.0, 0.0), axis=1) - 1.0
    wgt_to = jnp.sum(jnp.where(hit, wgt_t[None], 0.0), axis=1)
    idx = jnp.concatenate([row_to, wgt_to], axis=1)

    dma = pltpu.SemaphoreType.DMA
    vmem = pl.BlockSpec(memory_space=pltpu.VMEM)
    smem = pl.BlockSpec(memory_space=pltpu.SMEM)
    grad_up, place = pl.pallas_call(
        functools.partial(exchange_kernel, nz, nx, nh, tables, rows_dev),
        out_shape=(
            jax.ShapeDtypeStruct((out_rows, hid), F32),
            jax.ShapeDtypeStruct((slots, emb), F32),
        ),
        in_specs=[vmem] * 3,
        out_specs=(vmem, vmem),
        scratch_shapes=[
            pltpu.VMEM((nh, batch, width), BF16),
            pltpu.VMEM((n, batch, width), BF16),
            pltpu.VMEM((n, 2 * tables, batch), F32),
            pltpu.VMEM((nz, nx, out_rows, hid), BF16),
            pltpu.VMEM((nz, nx, out_rows, hid), BF16),
            pltpu.VMEM((nx, nz, out_rows, hid), BF16),
            pltpu.VMEM((nz, out_rows, hid), BF16),
            pltpu.VMEM((nz, out_rows, hid), BF16),
            dma((nh,)), dma((nh,)), dma((n,)), dma((n,)),
            dma((nz,)), dma((nz, nx)), dma((nz, nx)), dma((n,)),
            dma((nx,)), dma((nx,)), dma((nx,)), dma((nx,)), dma((nz,)), dma((nz,)),
        ],
        compiler_params=pltpu.CompilerParams(
            collective_id=0, has_side_effects=True, vmem_limit_bytes=60 * 1024 * 1024
        ),
        name="exchange",
    )(feat, grad, idx)

    chosen = evict_slots[0, 0]
    dest = evict_dest[0, 0]
    list_len = chosen.shape[0]
    cap = list_len // 2
    ids = jnp.arange(list_len, dtype=jnp.int32)
    live = ids < evict_count[0, 0]
    same = (dest[:, None] == dest[None, :]) & (ids[:, None] > ids[None, :]) & live[None, :]
    goal = jnp.where(live, dest * cap + jnp.sum(same.astype(jnp.int32), axis=1), nh * cap)

    new_weight, new_accum, send_rows, send_accum = pl.pallas_call(
        update_kernel,
        out_shape=(
            jax.ShapeDtypeStruct((slots, emb), F32),
            jax.ShapeDtypeStruct((slots // 128, 128), F32),
            jax.ShapeDtypeStruct((nh * cap + 8, emb), F32),
            jax.ShapeDtypeStruct((nh, cap), F32),
        ),
        in_specs=[smem] * 3 + [vmem] * 3,
        out_specs=(vmem,) * 4,
        scratch_shapes=[pltpu.VMEM((slots, emb), F32), pltpu.VMEM((slots, emb), F32)],
        name="update",
    )(
        slot_map.reshape(slots), chosen, goal.astype(jnp.int32), place,
        cache_weight.reshape(slots, emb), cache_accum.reshape(slots // 128, 128),
    )
    pad = -(-cap // emb)
    both = jnp.concatenate(
        [send_rows[: nh * cap].reshape(nh, cap, emb), send_accum.reshape(nh, pad, emb)], axis=1
    )
    both = lax.all_to_all(both, "hst", split_axis=0, concat_axis=0, tiled=True)
    return (
        grad_up,
        new_weight[None, None],
        new_accum.reshape(1, 1, slots),
        both[:, :cap][None, None],
        both[:, cap:].reshape(1, 1, nh, cap),
    )


def solution(mesh):
    n, nh = mesh.shape["tbl"], mesh.shape["hst"]
    nx = nh if n % (2 * nh) == 0 else 1
    nz = n // (2 * nx)
    placed = (
        P("tbl", None),
        P(None, "hst"),
        P("tbl", "hst"),
        P("hst", "tbl", None),
        P("hst", "tbl", None),
        P("hst", "tbl", None),
        P("hst", "tbl"),
        P("tbl", "hst", None),
        P("tbl", "hst", None, None),
        P("tbl", "hst", None),
        P("tbl", "hst", None),
        P("tbl", "hst", None),
        P("tbl", "hst"),
    )
    return jax.shard_map(
        functools.partial(on_device, nz, nx),
        mesh=mesh,
        in_specs=placed,
        out_specs=(
            P("tbl", "hst"),
            P("tbl", "hst", None, None),
            P("tbl", "hst", None),
            P("tbl", "hst", None, None, None),
            P("tbl", "hst", None, None),
        ),
        check_vma=False,
    )
```

```python
import functools

import jax
import jax.numpy as jnp
from jax import lax
from jax.experimental import pallas as pl
from jax.experimental.pallas import tpu as pltpu
from jax.sharding import PartitionSpec as P

LEARN_RATE = 0.05
EPSILON = 1e-08
MESH = pl.DeviceIdType.MESH
PIECES = 2
F32 = jnp.float32
BF16 = jnp.bfloat16


def exchange_kernel(
    nz, nx, nh, tables, rows_dev,
    feat, grad, idx,
    grad_out_ref, place_ref,
    ybuf, gat, idxb, rcore, a1, rx, a2, rz,
    y_s, y_r, i_s, i_r, azr_s, azl_s, ax_s, ac_s, g_r, rc_s, rc_r, rx_s, rx_r, rz_s, rz_r,
):
    n = nz * nx * 2
    me = lax.axis_index("tbl")
    h = lax.axis_index("hst")
    c = lax.rem(me, 2)
    zx = me // 2
    x = lax.rem(zx, nx)
    z = zx // nx
    other = 1 - c
    width = ybuf.shape[-1]
    emb = width // tables

    def at(zi, xi, ci):
        return (zi * nx + xi) * 2 + ci

    def zof(d):
        return lax.rem(z + d, nz)

    def xof(d):
        return lax.rem(x + d, nx)

    def rcopy(src, dst, s, r, dev):
        return pltpu.make_async_remote_copy(
            src_ref=src, dst_ref=dst, send_sem=s, recv_sem=r,
            device_id=dev, device_id_type=MESH,
        )

    barrier = pltpu.get_barrier_semaphore()

    def greet(d, carry):
        pl.semaphore_signal(
            barrier, inc=1, device_id={"tbl": lax.rem(me + d, n)}, device_id_type=MESH
        )
        return carry

    lax.fori_loop(1, n, greet, 0)
    for d in range(1, nh):
        pl.semaphore_signal(
            barrier, inc=1, device_id={"hst": lax.rem(h + d, nh)}, device_id_type=MESH
        )
    pl.semaphore_wait(barrier, n - 1 + nh - 1)

    def cols(hh):
        return pl.ds(pl.multiple_of(hh * width, width), width)

    batch = gat.shape[1]
    piece = batch // PIECES

    def span(k):
        return pl.ds(k * piece, piece)

    def y_copy(d, k):
        h2 = lax.rem(h + d, nh)
        return rcopy(
            feat.at[span(k), cols(h2)], ybuf.at[h, span(k)], y_s.at[d, k], y_r.at[h, k], {"hst": h2}
        )

    def y_arrival(d, k):
        h2 = lax.rem(h + d, nh)
        return rcopy(
            feat.at[span(k), cols(h2)], ybuf.at[h2, span(k)], y_s.at[d, k], y_r.at[h2, k],
            {"hst": h2},
        )

    def core_copy(x2):
        return rcopy(
            grad.at[:, x2, other], rcore.at[:, x2], rc_s.at[x2], rc_r.at[x2],
            {"tbl": at(z, x, other)},
        )

    def i_copy(d):
        o = lax.rem(me + d, n)
        return rcopy(idx.at[o], idxb.at[me], i_s.at[d], i_r.at[me], {"tbl": o})

    def i_arrival(slot):
        return rcopy(idx.at[slot], idxb.at[slot], i_s.at[0], i_r.at[slot], {"tbl": at(z, x, other)})

    for k in range(PIECES):
        for d in range(1, nh):
            y_copy(d, k).start()
    for d in range(1, nx + 1):
        core_copy(xof(d)).start()

    def i_start(d, carry):
        i_copy(d).start()
        return carry

    lax.fori_loop(1, n, i_start, 0)

    def rx_copy(d):
        x2 = xof(d)
        return rcopy(a1.at[:, x2], rx.at[x], rx_s.at[x2], rx_r.at[x], {"tbl": at(z, x2, c)})

    def rx_arrival(d):
        x2 = xof(d)
        return rcopy(a1.at[:, x2], rx.at[x2], rx_s.at[x2], rx_r.at[x2], {"tbl": at(z, x2, c)})

    for d in range(1, nx):
        x2 = xof(d)
        core_copy(x2).wait_recv()

        def add_core(k, carry):
            a1[k, x2] = (grad[k, x2, c] + rcore[k, x2]).astype(BF16)
            return carry

        lax.fori_loop(0, nz, add_core, 0)
        rx_copy(d).start()

    def g_copy(slot, k, sem, dev):
        ref = gat.at[slot, span(k)]
        return rcopy(ref, ref, sem, g_r.at[slot, k], {"tbl": dev})

    def right_copy(zi, k):
        return g_copy(at(zi, x, c), k, azr_s.at[zi, k], at(z + 1, x, c))

    def left_copy(zi, k):
        return g_copy(at(zi, x, c), k, azl_s.at[zi, k], at(z - 1, x, c))

    def x_copy(zi, d, k):
        return g_copy(at(zi, x, c), k, ax_s.at[zi, d, k], at(z, xof(d), c))

    def c_copy(zi, xi, k):
        return g_copy(at(zi, xi, c), k, ac_s.at[zi, xi, k], at(z, x, other))

    def arrived(slot, k):
        g_copy(slot, k, ac_s.at[0, 0, k], at(z, x, other)).wait_recv()

    for k in range(PIECES):
        for d in range(1, nh):
            y_arrival(d, k).wait_recv()
        total = feat[span(k), cols(h)].astype(F32)
        for d in range(1, nh):
            total = total + ybuf[lax.rem(h + d, nh), span(k)].astype(F32)
        gat[me, span(k)] = total.astype(BF16)

        @pl.when(z + 1 < nz)
        def _(k=k):
            right_copy(z, k).start()

        @pl.when(z >= 1)
        def _(k=k):
            left_copy(z, k).start()

        for d in range(1, nx):
            x_copy(z, d, k).start()
        c_copy(z, x, k).start()

    place_ref[...] = jnp.zeros_like(place_ref)
    idxb[me] = idx[me]
    chunk = min(256, rows_dev)

    def proc(slot):
        meta = idxb[slot]
        block = gat[slot]
        for t in range(tables):
            row = meta[t : t + 1, :]
            wgt = meta[tables + t : tables + t + 1, :]
            part = block[:, t * emb : (t + 1) * emb]
            for r0 in range(0, rows_dev, chunk):
                ids = lax.broadcasted_iota(jnp.int32, (chunk, batch), 0).astype(F32) + float(r0)
                mark = jnp.where(ids == row, wgt, 0.0).astype(BF16)
                place_ref[pl.ds(t * rows_dev + r0, chunk), :] += jnp.dot(
                    mark, part, preferred_element_type=F32
                )

    proc(me)

    def own_sum(k):
        s = grad[k, x, c] + rcore[k, x]
        for d in range(1, nx):
            s = s + rx[xof(d), k].astype(F32)
        return s

    def rz_copy(d):
        zi = zof(d)
        return rcopy(a2.at[zi], rz.at[z], rz_s.at[d], rz_r.at[z], {"tbl": at(zi, x, c)})

    def rz_arrival(d):
        zi = zof(d)
        return rcopy(a2.at[zi], rz.at[zi], rz_s.at[d], rz_r.at[zi], {"tbl": at(zi, x, c)})

    def rz_start(d, carry):
        zi = zof(d)
        a2[zi] = own_sum(zi).astype(BF16)
        rz_copy(d).start()
        return carry

    def from_z(zi, open_end, onward):
        slot = at(zi, x, c)
        for k in range(PIECES):
            arrived(slot, k)

            @pl.when(open_end)
            def _(k=k):
                onward(zi, k).start()

            for dx in range(1, nx):
                x_copy(zi, dx, k).start()
            c_copy(zi, x, k).start()
        i_arrival(slot).wait_recv()
        proc(slot)

    def from_x(zi):
        for dx in range(1, nx):
            slot = at(zi, xof(dx), c)
            for k in range(PIECES):
                arrived(slot, k)
                c_copy(zi, xof(dx), k).start()
            i_arrival(slot).wait_recv()
            proc(slot)

    def line_body(j, carry):
        @pl.when(z - j >= 0)
        def _():
            from_z(z - j, z + 1 < nz, right_copy)

        @pl.when(z + j < nz)
        def _():
            from_z(z + j, z >= 1, left_copy)

        @pl.when(j == (nz + 1) // 2)
        def _():
            core_copy(x).wait_recv()
            for d in range(1, nx):
                rx_arrival(d).wait_recv()
            lax.fori_loop(1, nz, rz_start, 0)

        @pl.when(z - j + 1 >= 0)
        def _():
            from_x(z - j + 1)

        @pl.when((j > 1) & (z + j - 1 < nz))
        def _():
            from_x(z + j - 1)

        return carry

    lax.fori_loop(1, nz + 1, line_body, 0)

    def c_body(k, carry):
        j = k // nz
        zi = zof(lax.rem(k, nz))
        slot = at(zi, xof(j), other)
        for p in range(PIECES):
            arrived(slot, p)
        i_arrival(slot).wait_recv()
        proc(slot)
        return carry

    lax.fori_loop(0, nz * nx, c_body, 0)

    grad_out_ref[...] = own_sum(z)

    def rz_end(d, carry):
        rz_arrival(d).wait_recv()
        grad_out_ref[...] += rz[zof(d)].astype(F32)
        return carry

    lax.fori_loop(1, nz, rz_end, 0)

    for p in range(PIECES):
        for d in range(1, nh):
            y_copy(d, p).wait_send()
    for d in range(1, nx + 1):
        core_copy(xof(d)).wait_send()
    for d in range(1, nx):
        rx_copy(d).wait_send()

    def i_end(d, carry):
        i_copy(d).wait_send()
        return carry

    lax.fori_loop(1, n, i_end, 0)

    def z_end(d, carry):
        rz_copy(d).wait_send()
        return carry

    lax.fori_loop(1, nz, z_end, 0)

    def end_all(k, carry):
        for p in range(PIECES):

            @pl.when((k <= z) & (z + 1 < nz))
            def _(p=p):
                right_copy(k, p).wait_send()

            @pl.when((k >= z) & (z >= 1))
            def _(p=p):
                left_copy(k, p).wait_send()

            for dx in range(1, nx):
                x_copy(k, dx, p).wait_send()
            for xi in range(nx):
                c_copy(k, xi, p).wait_send()
        return carry

    lax.fori_loop(0, nz, end_all, 0)


def update_kernel(
    slot_map, evict_slots, goal, place, weight, accum,
    new_weight, new_accum, send_rows, send_accum,
    sgrad, wide,
):
    slots = place.shape[0]
    list_len = evict_slots.shape[0]
    step = 16

    def scatter(i, carry):
        for j in range(step):
            r = i * step + j
            sgrad[pl.ds(slot_map[r], 1), :] = place[pl.ds(r, 1), :]
        return carry

    lax.fori_loop(0, slots // step, scatter, 0)
    tile = 128

    def adagrad(i, carry):
        at = pl.ds(i * tile, tile)
        g = sgrad[at, :]
        acc = accum[pl.ds(i, 1), :] + jnp.mean(g * g, axis=-1)[None, :]
        new_accum[pl.ds(i, 1), :] = acc
        col = jnp.broadcast_to(acc.reshape(tile, 1), g.shape)
        wide[at, :] = col
        new_weight[at, :] = weight[at, :] - LEARN_RATE * g / (jnp.sqrt(col) + EPSILON)
        return carry

    lax.fori_loop(0, slots // tile, adagrad, 0)
    send_rows[...] = jnp.zeros_like(send_rows)
    sgrad[...] = jnp.zeros_like(sgrad)

    def evict(i, carry):
        for j in range(8):
            p = i * 8 + j
            s = evict_slots[p]
            k = goal[p]
            send_rows[pl.ds(k, 1), :] = new_weight[pl.ds(s, 1), :]
            sgrad[pl.ds(k, 1), :] = wide[pl.ds(s, 1), :]
        return carry

    lax.fori_loop(0, list_len // 8, evict, 0)
    groups = send_accum.shape[0]
    cap = send_accum.shape[2]
    for d in range(groups):
        send_accum[d] = jnp.max(sgrad[d * cap : (d + 1) * cap, :], axis=-1)[None, :]


def hold_kernel(nh, rows, accum, held_rows, held_accum, rbuf, abuf, r_s, r_r, a_s, a_r):
    h = lax.axis_index("hst")
    cap = rbuf.shape[1]
    barrier = pltpu.get_barrier_semaphore()
    for d in range(1, nh):
        pl.semaphore_signal(
            barrier, inc=1, device_id={"hst": lax.rem(h + d, nh)}, device_id_type=MESH
        )
    pl.semaphore_wait(barrier, nh - 1)

    def part(k):
        return pl.ds(pl.multiple_of(k * cap, cap), cap)

    def copies(d, slot):
        k = lax.rem(h + d, nh)
        return [
            pltpu.make_async_remote_copy(
                src_ref=src, dst_ref=dst.at[slot], send_sem=s.at[d], recv_sem=r.at[slot],
                device_id={"hst": k}, device_id_type=MESH,
            )
            for src, dst, s, r in (
                (rows.at[part(k)], rbuf, r_s, r_r),
                (accum.at[k], abuf, a_s, a_r),
            )
        ]

    for d in range(1, nh):
        for copy in copies(d, h):
            copy.start()
    held_rows[h] = rows[part(h), :]
    held_accum[h] = accum[h]
    for d in range(1, nh):
        k = lax.rem(h + d, nh)
        for copy in copies(d, k):
            copy.wait_recv()
        held_rows[k] = rbuf[k]
        held_accum[k] = abuf[k]
    for d in range(1, nh):
        for copy in copies(d, h):
            copy.wait_send()


def on_device(
    nz, nx,
    pooled, w_up, grad_out, owners, rows, lookup_weight, lens, slot_map,
    cache_weight, cache_accum, evict_slots, evict_dest, evict_count,
):
    tables, batch, bag_len = owners.shape
    slots = slot_map.shape[-1]
    rows_dev = slots // tables
    emb = cache_weight.shape[-1]
    n = lax.axis_size("tbl")
    nh = lax.axis_size("hst")
    feat_n, hid = w_up.shape
    out_rows = feat_n // n
    width = tables * emb

    preact = jnp.dot(pooled, w_up, preferred_element_type=F32)
    sig = jax.nn.sigmoid(preact)
    delta = (grad_out.astype(F32) * sig * (1.0 + preact * (1.0 - sig))).astype(BF16)
    feat = lax.dot_general(
        delta, w_up, (((1,), (1,)), ((), ())), preferred_element_type=F32
    ).astype(BF16)
    grad = lax.dot_general(
        pooled, delta, (((0,), (0,)), ((), ())), preferred_element_type=F32
    )
    grad = grad.reshape(nz, nx, 2, out_rows, hid)

    own_t = jnp.transpose(owners, (2, 0, 1))
    row_t = jnp.transpose(rows, (2, 0, 1)).astype(F32)
    wgt_t = jnp.transpose(lookup_weight, (2, 0, 1)).astype(F32)
    used = jnp.arange(bag_len, dtype=jnp.int32)[:, None, None] < lens[None]
    hit = (own_t[None] == jnp.arange(n, dtype=jnp.int32)[:, None, None, None]) & used[None]
    row_to = jnp.sum(jnp.where(hit, row_t[None] + 1.0, 0.0), axis=1) - 1.0
    wgt_to = jnp.sum(jnp.where(hit, wgt_t[None], 0.0), axis=1)
    idx = jnp.concatenate([row_to, wgt_to], axis=1)

    dma = pltpu.SemaphoreType.DMA
    vmem = pl.BlockSpec(memory_space=pltpu.VMEM)
    smem = pl.BlockSpec(memory_space=pltpu.SMEM)
    grad_up, place = pl.pallas_call(
        functools.partial(exchange_kernel, nz, nx, nh, tables, rows_dev),
        out_shape=(
            jax.ShapeDtypeStruct((out_rows, hid), F32),
            jax.ShapeDtypeStruct((slots, emb), F32),
        ),
        in_specs=[vmem] * 3,
        out_specs=(vmem, vmem),
        scratch_shapes=[
            pltpu.VMEM((nh, batch, width), BF16),
            pltpu.VMEM((n, batch, width), BF16),
            pltpu.VMEM((n, 2 * tables, batch), F32),
            pltpu.VMEM((nz, nx, out_rows, hid), F32),
            pltpu.VMEM((nz, nx, out_rows, hid), BF16),
            pltpu.VMEM((nx, nz, out_rows, hid), BF16),
            pltpu.VMEM((nz, out_rows, hid), BF16),
            pltpu.VMEM((nz, out_rows, hid), BF16),
            dma((nh, PIECES)), dma((nh, PIECES)), dma((n,)), dma((n,)),
            dma((nz, PIECES)), dma((nz, PIECES)), dma((nz, nx, PIECES)), dma((nz, nx, PIECES)),
            dma((n, PIECES)),
            dma((nx,)), dma((nx,)), dma((nx,)), dma((nx,)), dma((nz,)), dma((nz,)),
        ],
        compiler_params=pltpu.CompilerParams(
            collective_id=0, has_side_effects=True, vmem_limit_bytes=60 * 1024 * 1024
        ),
        name="exchange",
    )(feat, grad, idx)

    chosen = evict_slots[0, 0]
    dest = evict_dest[0, 0]
    list_len = chosen.shape[0]
    cap = list_len // 2
    ids = jnp.arange(list_len, dtype=jnp.int32)
    live = ids < evict_count[0, 0]
    same = (dest[:, None] == dest[None, :]) & (ids[:, None] > ids[None, :]) & live[None, :]
    goal = jnp.where(live, dest * cap + jnp.sum(same.astype(jnp.int32), axis=1), nh * cap)

    new_weight, new_accum, send_rows, send_accum = pl.pallas_call(
        update_kernel,
        out_shape=(
            jax.ShapeDtypeStruct((slots, emb), F32),
            jax.ShapeDtypeStruct((slots // 128, 128), F32),
            jax.ShapeDtypeStruct((nh * cap + 8, emb), F32),
            jax.ShapeDtypeStruct((nh, 1, cap), F32),
        ),
        in_specs=[smem] * 3 + [vmem] * 3,
        out_specs=(vmem,) * 4,
        scratch_shapes=[pltpu.VMEM((slots, emb), F32), pltpu.VMEM((slots, emb), F32)],
        name="update",
    )(
        slot_map.reshape(slots), chosen, goal.astype(jnp.int32), place,
        cache_weight.reshape(slots, emb), cache_accum.reshape(slots // 128, 128),
    )
    held_rows, held_accum = pl.pallas_call(
        functools.partial(hold_kernel, nh),
        out_shape=(
            jax.ShapeDtypeStruct((nh, cap, emb), F32),
            jax.ShapeDtypeStruct((nh, 1, cap), F32),
        ),
        in_specs=[vmem, vmem],
        out_specs=(vmem, vmem),
        scratch_shapes=[
            pltpu.VMEM((nh, cap, emb), F32),
            pltpu.VMEM((nh, 1, cap), F32),
            dma((nh,)), dma((nh,)), dma((nh,)), dma((nh,)),
        ],
        compiler_params=pltpu.CompilerParams(collective_id=1, has_side_effects=True),
        name="hold",
    )(send_rows, send_accum)
    return (
        grad_up,
        new_weight[None, None],
        new_accum.reshape(1, 1, slots),
        held_rows[None, None],
        held_accum.reshape(1, 1, nh, cap),
    )


def solution(mesh):
    n, nh = mesh.shape["tbl"], mesh.shape["hst"]
    nx = nh if n % (2 * nh) == 0 else 1
    nz = n // (2 * nx)
    placed = (
        P("tbl", None),
        P(None, "hst"),
        P("tbl", "hst"),
        P("hst", "tbl", None),
        P("hst", "tbl", None),
        P("hst", "tbl", None),
        P("hst", "tbl"),
        P("tbl", "hst", None),
        P("tbl", "hst", None, None),
        P("tbl", "hst", None),
        P("tbl", "hst", None),
        P("tbl", "hst", None),
        P("tbl", "hst"),
    )
    return jax.shard_map(
        functools.partial(on_device, nz, nx),
        mesh=mesh,
        in_specs=placed,
        out_specs=(
            P("tbl", "hst"),
            P("tbl", "hst", None, None),
            P("tbl", "hst", None),
            P("tbl", "hst", None, None, None),
            P("tbl", "hst", None, None),
        ),
        check_vma=False,
    )
```

```python
import functools

import jax
import jax.numpy as jnp
from jax import lax
from jax.experimental import pallas as pl
from jax.experimental.pallas import tpu as pltpu
from jax.sharding import PartitionSpec as P

LEARN_RATE = 0.05
EPSILON = 1e-08
MESH = pl.DeviceIdType.MESH
PIECES = 4
F32 = jnp.float32
BF16 = jnp.bfloat16


def exchange_kernel(
    nz, nx, nh, tables, rows_dev,
    feat, grad, idx,
    grad_out_ref, place_ref,
    ybuf, gat, idxb, rcore, a1, rx, a2, rz,
    y_s, y_r, i_s, i_r, azr_s, azl_s, ax_s, ac_s, g_r, rc_s, rc_r, rx_s, rx_r, rz_s, rz_r,
):
    n = nz * nx * 2
    me = lax.axis_index("tbl")
    h = lax.axis_index("hst")
    c = lax.rem(me, 2)
    zx = me // 2
    x = lax.rem(zx, nx)
    z = zx // nx
    other = 1 - c
    width = ybuf.shape[-1]
    emb = width // tables

    def at(zi, xi, ci):
        return (zi * nx + xi) * 2 + ci

    def zof(d):
        return lax.rem(z + d, nz)

    def xof(d):
        return lax.rem(x + d, nx)

    def rcopy(src, dst, s, r, dev):
        return pltpu.make_async_remote_copy(
            src_ref=src, dst_ref=dst, send_sem=s, recv_sem=r,
            device_id=dev, device_id_type=MESH,
        )

    barrier = pltpu.get_barrier_semaphore()

    def greet(d, carry):
        pl.semaphore_signal(
            barrier, inc=1, device_id={"tbl": lax.rem(me + d, n)}, device_id_type=MESH
        )
        return carry

    lax.fori_loop(1, n, greet, 0)
    for d in range(1, nh):
        pl.semaphore_signal(
            barrier, inc=1, device_id={"hst": lax.rem(h + d, nh)}, device_id_type=MESH
        )
    pl.semaphore_wait(barrier, n - 1 + nh - 1)

    def cols(hh):
        return pl.ds(pl.multiple_of(hh * width, width), width)

    batch = gat.shape[1]
    piece = batch // PIECES

    def span(k):
        return pl.ds(k * piece, piece)

    def y_copy(d, k):
        h2 = lax.rem(h + d, nh)
        return rcopy(
            feat.at[span(k), cols(h2)], ybuf.at[h, span(k)], y_s.at[d, k], y_r.at[h, k], {"hst": h2}
        )

    def y_arrival(d, k):
        h2 = lax.rem(h + d, nh)
        return rcopy(
            feat.at[span(k), cols(h2)], ybuf.at[h2, span(k)], y_s.at[d, k], y_r.at[h2, k],
            {"hst": h2},
        )

    def core_copy(x2):
        return rcopy(
            grad.at[:, x2, other], rcore.at[:, x2], rc_s.at[x2], rc_r.at[x2],
            {"tbl": at(z, x, other)},
        )

    def i_copy(d):
        o = lax.rem(me + d, n)
        return rcopy(idx.at[o], idxb.at[me], i_s.at[d], i_r.at[me], {"tbl": o})

    def i_arrival(slot):
        return rcopy(idx.at[slot], idxb.at[slot], i_s.at[0], i_r.at[slot], {"tbl": at(z, x, other)})

    for k in range(PIECES):
        for d in range(1, nh):
            y_copy(d, k).start()
    for d in range(1, nx + 1):
        core_copy(xof(d)).start()

    def i_start(d, carry):
        i_copy(d).start()
        return carry

    lax.fori_loop(1, n, i_start, 0)

    def rx_copy(d):
        x2 = xof(d)
        return rcopy(a1.at[:, x2], rx.at[x], rx_s.at[x2], rx_r.at[x], {"tbl": at(z, x2, c)})

    def rx_arrival(d):
        x2 = xof(d)
        return rcopy(a1.at[:, x2], rx.at[x2], rx_s.at[x2], rx_r.at[x2], {"tbl": at(z, x2, c)})

    for d in range(1, nx):
        x2 = xof(d)
        core_copy(x2).wait_recv()

        def add_core(k, carry):
            a1[k, x2] = (grad[k, x2, c] + rcore[k, x2]).astype(BF16)
            return carry

        lax.fori_loop(0, nz, add_core, 0)
        rx_copy(d).start()

    def g_copy(slot, k, sem, dev):
        ref = gat.at[slot, span(k)]
        return rcopy(ref, ref, sem, g_r.at[slot, k], {"tbl": dev})

    def right_copy(zi, k):
        return g_copy(at(zi, x, c), k, azr_s.at[zi, k], at(z + 1, x, c))

    def left_copy(zi, k):
        return g_copy(at(zi, x, c), k, azl_s.at[zi, k], at(z - 1, x, c))

    def x_copy(zi, d, k):
        return g_copy(at(zi, x, c), k, ax_s.at[zi, d, k], at(z, xof(d), c))

    def c_copy(zi, xi, k):
        return g_copy(at(zi, xi, c), k, ac_s.at[zi, xi, k], at(z, x, other))

    def arrived(slot, k):
        g_copy(slot, k, ac_s.at[0, 0, k], at(z, x, other)).wait_recv()

    for k in range(PIECES):
        for d in range(1, nh):
            y_arrival(d, k).wait_recv()
        total = feat[span(k), cols(h)].astype(F32)
        for d in range(1, nh):
            total = total + ybuf[lax.rem(h + d, nh), span(k)].astype(F32)
        gat[me, span(k)] = total.astype(BF16)

        @pl.when(z + 1 < nz)
        def _(k=k):
            right_copy(z, k).start()

        @pl.when(z >= 1)
        def _(k=k):
            left_copy(z, k).start()

        for d in range(1, nx):
            x_copy(z, d, k).start()
        c_copy(z, x, k).start()

    place_ref[...] = jnp.zeros_like(place_ref)
    idxb[me] = idx[me]
    chunk = min(256, rows_dev)

    def proc(slot):
        meta = idxb[slot]
        block = gat[slot]
        for t in range(tables):
            row = meta[t : t + 1, :]
            wgt = meta[tables + t : tables + t + 1, :]
            part = block[:, t * emb : (t + 1) * emb]
            for r0 in range(0, rows_dev, chunk):
                ids = lax.broadcasted_iota(jnp.int32, (chunk, batch), 0).astype(F32) + float(r0)
                mark = jnp.where(ids == row, wgt, 0.0).astype(BF16)
                place_ref[pl.ds(t * rows_dev + r0, chunk), :] += jnp.dot(
                    mark, part, preferred_element_type=F32
                )

    proc(me)

    def own_sum(k):
        s = grad[k, x, c] + rcore[k, x]
        for d in range(1, nx):
            s = s + rx[xof(d), k].astype(F32)
        return s

    def rz_copy(d):
        zi = zof(d)
        return rcopy(a2.at[zi], rz.at[z], rz_s.at[d], rz_r.at[z], {"tbl": at(zi, x, c)})

    def rz_arrival(d):
        zi = zof(d)
        return rcopy(a2.at[zi], rz.at[zi], rz_s.at[d], rz_r.at[zi], {"tbl": at(zi, x, c)})

    def rz_start(d, carry):
        zi = zof(d)
        a2[zi] = own_sum(zi).astype(BF16)
        rz_copy(d).start()
        return carry

    def from_z(zi, open_end, onward):
        slot = at(zi, x, c)
        for k in range(PIECES):
            arrived(slot, k)

            @pl.when(open_end)
            def _(k=k):
                onward(zi, k).start()

            for dx in range(1, nx):
                x_copy(zi, dx, k).start()
            c_copy(zi, x, k).start()
        i_arrival(slot).wait_recv()
        proc(slot)

    def from_x(zi):
        for dx in range(1, nx):
            slot = at(zi, xof(dx), c)
            for k in range(PIECES):
                arrived(slot, k)
                c_copy(zi, xof(dx), k).start()
            i_arrival(slot).wait_recv()
            proc(slot)

    def line_body(j, carry):
        @pl.when(z - j >= 0)
        def _():
            from_z(z - j, z + 1 < nz, right_copy)

        @pl.when(z + j < nz)
        def _():
            from_z(z + j, z >= 1, left_copy)

        @pl.when(j == (nz + 1) // 2)
        def _():
            core_copy(x).wait_recv()
            for d in range(1, nx):
                rx_arrival(d).wait_recv()
            lax.fori_loop(1, nz, rz_start, 0)

        @pl.when(z - j + 1 >= 0)
        def _():
            from_x(z - j + 1)

        @pl.when((j > 1) & (z + j - 1 < nz))
        def _():
            from_x(z + j - 1)

        return carry

    lax.fori_loop(1, nz + 1, line_body, 0)

    def c_body(k, carry):
        j = k // nz
        zi = zof(lax.rem(k, nz))
        slot = at(zi, xof(j), other)
        for p in range(PIECES):
            arrived(slot, p)
        i_arrival(slot).wait_recv()
        proc(slot)
        return carry

    lax.fori_loop(0, nz * nx, c_body, 0)

    grad_out_ref[...] = own_sum(z)

    def rz_end(d, carry):
        rz_arrival(d).wait_recv()
        grad_out_ref[...] += rz[zof(d)].astype(F32)
        return carry

    lax.fori_loop(1, nz, rz_end, 0)

    for p in range(PIECES):
        for d in range(1, nh):
            y_copy(d, p).wait_send()
    for d in range(1, nx + 1):
        core_copy(xof(d)).wait_send()
    for d in range(1, nx):
        rx_copy(d).wait_send()

    def i_end(d, carry):
        i_copy(d).wait_send()
        return carry

    lax.fori_loop(1, n, i_end, 0)

    def z_end(d, carry):
        rz_copy(d).wait_send()
        return carry

    lax.fori_loop(1, nz, z_end, 0)

    def end_all(k, carry):
        for p in range(PIECES):

            @pl.when((k <= z) & (z + 1 < nz))
            def _(p=p):
                right_copy(k, p).wait_send()

            @pl.when((k >= z) & (z >= 1))
            def _(p=p):
                left_copy(k, p).wait_send()

            for dx in range(1, nx):
                x_copy(k, dx, p).wait_send()
            for xi in range(nx):
                c_copy(k, xi, p).wait_send()
        return carry

    lax.fori_loop(0, nz, end_all, 0)


def update_kernel(
    slot_map, evict_slots, goal, place, weight, accum,
    new_weight, new_accum, send_rows, send_accum,
    sgrad, wide,
):
    slots = place.shape[0]
    list_len = evict_slots.shape[0]
    step = 16

    def scatter(i, carry):
        for j in range(step):
            r = i * step + j
            sgrad[pl.ds(slot_map[r], 1), :] = place[pl.ds(r, 1), :]
        return carry

    lax.fori_loop(0, slots // step, scatter, 0)
    tile = 128

    def adagrad(i, carry):
        at = pl.ds(i * tile, tile)
        g = sgrad[at, :]
        acc = accum[pl.ds(i, 1), :] + jnp.mean(g * g, axis=-1)[None, :]
        new_accum[pl.ds(i, 1), :] = acc
        col = jnp.broadcast_to(acc.reshape(tile, 1), g.shape)
        wide[at, :] = col
        new_weight[at, :] = weight[at, :] - LEARN_RATE * g / (jnp.sqrt(col) + EPSILON)
        return carry

    lax.fori_loop(0, slots // tile, adagrad, 0)
    send_rows[...] = jnp.zeros_like(send_rows)
    sgrad[...] = jnp.zeros_like(sgrad)

    def evict(i, carry):
        for j in range(8):
            p = i * 8 + j
            s = evict_slots[p]
            k = goal[p]
            send_rows[pl.ds(k, 1), :] = new_weight[pl.ds(s, 1), :]
            sgrad[pl.ds(k, 1), :] = wide[pl.ds(s, 1), :]
        return carry

    lax.fori_loop(0, list_len // 8, evict, 0)
    groups = send_accum.shape[0]
    cap = send_accum.shape[2]
    for d in range(groups):
        send_accum[d] = jnp.max(sgrad[d * cap : (d + 1) * cap, :], axis=-1)[None, :]


def hold_kernel(nh, rows, accum, held_rows, held_accum, rbuf, abuf, r_s, r_r, a_s, a_r):
    h = lax.axis_index("hst")
    cap = rbuf.shape[1]
    barrier = pltpu.get_barrier_semaphore()
    for d in range(1, nh):
        pl.semaphore_signal(
            barrier, inc=1, device_id={"hst": lax.rem(h + d, nh)}, device_id_type=MESH
        )
    pl.semaphore_wait(barrier, nh - 1)

    def part(k):
        return pl.ds(pl.multiple_of(k * cap, cap), cap)

    def copies(d, slot):
        k = lax.rem(h + d, nh)
        return [
            pltpu.make_async_remote_copy(
                src_ref=src, dst_ref=dst.at[slot], send_sem=s.at[d], recv_sem=r.at[slot],
                device_id={"hst": k}, device_id_type=MESH,
            )
            for src, dst, s, r in (
                (rows.at[part(k)], rbuf, r_s, r_r),
                (accum.at[k], abuf, a_s, a_r),
            )
        ]

    for d in range(1, nh):
        for copy in copies(d, h):
            copy.start()
    held_rows[h] = rows[part(h), :]
    held_accum[h] = accum[h]
    for d in range(1, nh):
        k = lax.rem(h + d, nh)
        for copy in copies(d, k):
            copy.wait_recv()
        held_rows[k] = rbuf[k]
        held_accum[k] = abuf[k]
    for d in range(1, nh):
        for copy in copies(d, h):
            copy.wait_send()


def on_device(
    nz, nx,
    pooled, w_up, grad_out, owners, rows, lookup_weight, lens, slot_map,
    cache_weight, cache_accum, evict_slots, evict_dest, evict_count,
):
    tables, batch, bag_len = owners.shape
    slots = slot_map.shape[-1]
    rows_dev = slots // tables
    emb = cache_weight.shape[-1]
    n = lax.axis_size("tbl")
    nh = lax.axis_size("hst")
    feat_n, hid = w_up.shape
    out_rows = feat_n // n
    width = tables * emb

    preact = jnp.dot(pooled, w_up, preferred_element_type=F32)
    sig = jax.nn.sigmoid(preact)
    delta = (grad_out.astype(F32) * sig * (1.0 + preact * (1.0 - sig))).astype(BF16)
    feat = lax.dot_general(
        delta, w_up, (((1,), (1,)), ((), ())), preferred_element_type=F32
    ).astype(BF16)
    grad = lax.dot_general(
        pooled, delta, (((0,), (0,)), ((), ())), preferred_element_type=F32
    )
    grad = grad.reshape(nz, nx, 2, out_rows, hid)

    own_t = jnp.transpose(owners, (2, 0, 1))
    row_t = jnp.transpose(rows, (2, 0, 1)).astype(F32)
    wgt_t = jnp.transpose(lookup_weight, (2, 0, 1)).astype(F32)
    used = jnp.arange(bag_len, dtype=jnp.int32)[:, None, None] < lens[None]
    hit = (own_t[None] == jnp.arange(n, dtype=jnp.int32)[:, None, None, None]) & used[None]
    row_to = jnp.sum(jnp.where(hit, row_t[None] + 1.0, 0.0), axis=1) - 1.0
    wgt_to = jnp.sum(jnp.where(hit, wgt_t[None], 0.0), axis=1)
    idx = jnp.concatenate([row_to, wgt_to], axis=1)

    dma = pltpu.SemaphoreType.DMA
    vmem = pl.BlockSpec(memory_space=pltpu.VMEM)
    smem = pl.BlockSpec(memory_space=pltpu.SMEM)
    grad_up, place = pl.pallas_call(
        functools.partial(exchange_kernel, nz, nx, nh, tables, rows_dev),
        out_shape=(
            jax.ShapeDtypeStruct((out_rows, hid), F32),
            jax.ShapeDtypeStruct((slots, emb), F32),
        ),
        in_specs=[vmem] * 3,
        out_specs=(vmem, vmem),
        scratch_shapes=[
            pltpu.VMEM((nh, batch, width), BF16),
            pltpu.VMEM((n, batch, width), BF16),
            pltpu.VMEM((n, 2 * tables, batch), F32),
            pltpu.VMEM((nz, nx, out_rows, hid), F32),
            pltpu.VMEM((nz, nx, out_rows, hid), BF16),
            pltpu.VMEM((nx, nz, out_rows, hid), BF16),
            pltpu.VMEM((nz, out_rows, hid), BF16),
            pltpu.VMEM((nz, out_rows, hid), BF16),
            dma((nh, PIECES)), dma((nh, PIECES)), dma((n,)), dma((n,)),
            dma((nz, PIECES)), dma((nz, PIECES)), dma((nz, nx, PIECES)), dma((nz, nx, PIECES)),
            dma((n, PIECES)),
            dma((nx,)), dma((nx,)), dma((nx,)), dma((nx,)), dma((nz,)), dma((nz,)),
        ],
        compiler_params=pltpu.CompilerParams(
            collective_id=0, has_side_effects=True, vmem_limit_bytes=60 * 1024 * 1024
        ),
        name="exchange",
    )(feat, grad, idx)

    chosen = evict_slots[0, 0]
    dest = evict_dest[0, 0]
    list_len = chosen.shape[0]
    cap = list_len // 2
    ids = jnp.arange(list_len, dtype=jnp.int32)
    live = ids < evict_count[0, 0]
    same = (dest[:, None] == dest[None, :]) & (ids[:, None] > ids[None, :]) & live[None, :]
    goal = jnp.where(live, dest * cap + jnp.sum(same.astype(jnp.int32), axis=1), nh * cap)

    new_weight, new_accum, send_rows, send_accum = pl.pallas_call(
        update_kernel,
        out_shape=(
            jax.ShapeDtypeStruct((slots, emb), F32),
            jax.ShapeDtypeStruct((slots // 128, 128), F32),
            jax.ShapeDtypeStruct((nh * cap + 8, emb), F32),
            jax.ShapeDtypeStruct((nh, 1, cap), F32),
        ),
        in_specs=[smem] * 3 + [vmem] * 3,
        out_specs=(vmem,) * 4,
        scratch_shapes=[pltpu.VMEM((slots, emb), F32), pltpu.VMEM((slots, emb), F32)],
        name="update",
    )(
        slot_map.reshape(slots), chosen, goal.astype(jnp.int32), place,
        cache_weight.reshape(slots, emb), cache_accum.reshape(slots // 128, 128),
    )
    held_rows, held_accum = pl.pallas_call(
        functools.partial(hold_kernel, nh),
        out_shape=(
            jax.ShapeDtypeStruct((nh, cap, emb), F32),
            jax.ShapeDtypeStruct((nh, 1, cap), F32),
        ),
        in_specs=[vmem, vmem],
        out_specs=(vmem, vmem),
        scratch_shapes=[
            pltpu.VMEM((nh, cap, emb), F32),
            pltpu.VMEM((nh, 1, cap), F32),
            dma((nh,)), dma((nh,)), dma((nh,)), dma((nh,)),
        ],
        compiler_params=pltpu.CompilerParams(collective_id=1, has_side_effects=True),
        name="hold",
    )(send_rows, send_accum)
    return (
        grad_up,
        new_weight[None, None],
        new_accum.reshape(1, 1, slots),
        held_rows[None, None],
        held_accum.reshape(1, 1, nh, cap),
    )


def solution(mesh):
    n, nh = mesh.shape["tbl"], mesh.shape["hst"]
    nx = nh if n % (2 * nh) == 0 else 1
    nz = n // (2 * nx)
    placed = (
        P("tbl", None),
        P(None, "hst"),
        P("tbl", "hst"),
        P("hst", "tbl", None),
        P("hst", "tbl", None),
        P("hst", "tbl", None),
        P("hst", "tbl"),
        P("tbl", "hst", None),
        P("tbl", "hst", None, None),
        P("tbl", "hst", None),
        P("tbl", "hst", None),
        P("tbl", "hst", None),
        P("tbl", "hst"),
    )
    return jax.shard_map(
        functools.partial(on_device, nz, nx),
        mesh=mesh,
        in_specs=placed,
        out_specs=(
            P("tbl", "hst"),
            P("tbl", "hst", None, None),
            P("tbl", "hst", None),
            P("tbl", "hst", None, None, None),
            P("tbl", "hst", None, None),
        ),
        check_vma=False,
    )
```
